32 devices in a mesh: dp: 4 (over z), expert: 8 (over y, x, core).
Axes of the slice: x: 2, y: 2, z: 4, core: 2. Of those that a mesh axis runs over, the one named last changes fastest.
Arguments:
- tokens: bfloat16 [4096, 4096], P(('dp', 'expert')), may hold values from -6 to 6
- expert_ids: int32 [4096, 2], P(('dp', 'expert')), may hold values from 0 to 7, all different within a row; in each aligned block of 128 rows (0 to 127, 128 to 255, ...) at most 36 rows name the same one
- router_probs: float32 [4096, 2], P(('dp', 'expert')), may hold values from 0.1 to 1
- w_gate: bfloat16 [8, 1024, 4096], P('expert', 'dp'), may hold values from -0.09375 to 0.09375
- w_up: bfloat16 [8, 1024, 4096], P('expert', 'dp'), may hold values from -0.09375 to 0.09375
- w_down: bfloat16 [8, 1024, 4096], P('expert', 'dp'), may hold values from -0.1875 to 0.1875
- out_grad: bfloat16 [4096, 4096], P(('dp', 'expert')), may hold values from -6 to 6
Outputs:
- mixed: bfloat16 [4096, 4096], P(('dp', 'expert'))
- input_grad: bfloat16 [4096, 4096], P(('dp', 'expert'))
- prob_grad: float32 [4096, 2], P(('dp', 'expert'))
- grad_gate: bfloat16 [8, 1024, 4096], P('expert', 'dp')
- grad_up: bfloat16 [8, 1024, 4096], P('expert', 'dp')
- grad_down: bfloat16 [8, 1024, 4096], P('expert', 'dp')
The draws below stay inside these ranges and needn't reach their ends.
Inputs may be any that keep to these rules, and one draw needn't show every extreme that they name: `expert_ids`: each row names 2 different experts. Among the rows of one device no expert is named more than 36 times, a bound that some block reaches.
All inputs are finite; a program needn't handle non-finite values.
Results may differ from the reference program's by a relative error of at most 0.018.
Values may be sent and summed in bfloat16 or wider, within the bound.
A program may use at most 192 MiB of HBM per device.

```python
import math
import jax
import jax.numpy as jnp
import numpy as np
from jax import lax

D = 4096
FFW = 1024
TOPK = 2
TOK_DEV = 128
EXPERTS = 8
MOST = 36
TOKENS = 4096
N_DP = 4
N_EXPERT = 8


def steps_of(own_key, dims, split, low, top_value):
    level, own = 1.0, jax.random.fold_in(own_key, 6)
    for axis_at, shards_of in split:
        steps = jnp.exp(jax.random.uniform(jax.random.fold_in(own, axis_at), (shards_of,), jnp.float32, low / len(split), top_value / len(split)))
        level = level * jnp.repeat(steps, dims[axis_at] // shards_of).reshape([-1 if axis == axis_at else 1 for axis in range(len(dims))])
    return level


def assign_block(key, own, number, rows, count, top, most, skew):
    ranking = jax.random.permutation(key, count)
    packed, common = load_shares(count, rows * top, most, skew, True), load_shares(count, rows * top, most, skew, False)
    places = jnp.arange(count)

    def named(lengths, turn):
        used = int((lengths > 0).sum())
        fixed = max(1, used // 4)
        passed = fixed + (places - fixed + turn * (used - fixed)) % max(1, count - fixed)
        return jnp.zeros((count,), jnp.int32).at[ranking[jnp.where(places < fixed, places, passed)]].set(jnp.asarray(lengths, jnp.int32))

    lengths = jnp.where(number % 4 == 0, named(packed, number // 4), named(common, number - number // 4 - 1))
    mixed = jax.random.permutation(jax.random.fold_in(own, 3), count)
    donor, receiver = mixed[0:count // 2 * 2:2], mixed[1:count // 2 * 2:2]
    margin = jnp.minimum(lengths[donor] - 1, most - lengths[receiver]) // 2
    margin = jnp.where((donor == ranking[0]) | (receiver == ranking[0]) | (lengths[receiver] == 0), 0, jnp.maximum(margin, 0))
    passed = jax.random.randint(jax.random.fold_in(own, 4), (count // 2,), 0, 1 << 20) % (margin + 1)
    lengths = lengths.at[donor].add(-passed).at[receiver].add(passed)
    items = jnp.searchsorted(jnp.cumsum(lengths), jnp.arange(rows * top), side="right").astype(jnp.int32)
    listing = items.reshape(top, rows).T
    listing = listing[jax.random.permutation(jax.random.fold_in(own, 1), rows)]
    turn = jax.random.randint(jax.random.fold_in(own, 2), (rows, 1), 0, top)
    return jnp.take_along_axis(listing, (jnp.arange(top)[None, :] + turn) % top, axis=1)


def load_shares(count, total, limit, lean, full):
    loads = [(1 << 20) // math.isqrt(rank ** lean) + 1 for rank in range(1, count + 1)]
    largest = limit if full else min(limit, max(-(-total // count), total * loads[0] // sum(loads)))
    least = 1 if total - largest >= count - 1 else 0
    counts, spare = [largest] + [least] * (count - 1), total - largest - least * (count - 1)
    while spare > 0:
        movable = [i for i in range(1, count) if counts[i] < largest] or [i for i in range(1, count) if counts[i] < limit]
        mass, remaining = sum([loads[i] for i in movable]), spare
        for i in movable:
            extra = min(limit - counts[i], max(1, remaining * loads[i] // mass), spare)
            counts[i] = counts[i] + extra
            spare = spare - extra
    return np.array(counts)


def bell_draw(key, dims, width, limit, pieces=(), kind=jnp.bfloat16):
    drawn = width * jax.random.normal(key, dims, jnp.float32)
    if pieces:
        drawn = drawn * steps_of(key, dims, pieces, -0.22, 0.18)
    return jnp.clip(drawn, -limit, limit).astype(kind)


def setup_inputs(seed: int = 0) -> dict:
    splits = jax.random.split(jax.random.key(seed), 8)
    tokens = bell_draw(splits[0], (TOKENS, D), 1.0, 6.0, ((0, 32),))
    expert_ids_keys = jax.random.split(jax.random.fold_in(splits[1], 1), TOKENS // TOK_DEV)
    expert_ids_turns = jax.random.permutation(jax.random.fold_in(splits[1], 3), TOKENS // TOK_DEV)
    expert_ids = jax.vmap(lambda own, number: assign_block(jax.random.fold_in(splits[1], 2), own, number, TOK_DEV, EXPERTS, TOPK, MOST, 2))(expert_ids_keys, expert_ids_turns).reshape((TOKENS, TOPK))
    router_probs = jnp.clip(0.1 + 0.9 * jax.random.uniform(splits[2], (TOKENS, TOPK), jnp.float32) ** steps_of(splits[2], (TOKENS, TOPK), ((0, 32),), -0.2, 0.2), 0.1, 1.0)
    w_gate = bell_draw(splits[3], (EXPERTS, FFW, D), D ** -0.5, 0.09375, ((0, 8), (1, 4)))
    w_up = bell_draw(splits[4], (EXPERTS, FFW, D), D ** -0.5, 0.09375, ((0, 8), (1, 4)))
    w_down = bell_draw(splits[5], (EXPERTS, FFW, D), FFW ** -0.5, 0.1875, ((0, 8), (1, 4)))
    out_grad = bell_draw(splits[6], (TOKENS, D), 1.0, 6.0, ((0, 32),))
    return dict(tokens=tokens, expert_ids=expert_ids, router_probs=router_probs, w_gate=w_gate, w_up=w_up, w_down=w_down, out_grad=out_grad)


def expert_pass(tok_slots, grad_slots, gate_w, up_w, down_w):
    gate_proj = jnp.dot(tok_slots, gate_w.T, preferred_element_type=jnp.float32)
    up_proj = jnp.dot(tok_slots, up_w.T, preferred_element_type=jnp.float32)
    sigmoid_gate = jax.nn.sigmoid(gate_proj)
    activated = gate_proj * sigmoid_gate
    hidden = (activated * up_proj).astype(jnp.bfloat16)
    d_hidden = jnp.dot(grad_slots, down_w.T, preferred_element_type=jnp.float32)
    d_gate = (d_hidden * up_proj * sigmoid_gate * (1.0 + gate_proj * (1.0 - sigmoid_gate))).astype(jnp.bfloat16)
    d_up = (d_hidden * activated).astype(jnp.bfloat16)
    quarter_width = FFW // N_DP
    out_sum = jnp.zeros((tok_slots.shape[0], D), jnp.float32)
    back_sum = jnp.zeros((tok_slots.shape[0], D), jnp.float32)
    for part_index in range(N_DP):
        lower = part_index * quarter_width
        upper = lower + quarter_width
        part_out = jnp.dot(hidden[:, lower:upper], down_w[lower:upper], preferred_element_type=jnp.float32)
        part_out = lax.optimization_barrier(part_out.astype(jnp.bfloat16))
        out_sum = out_sum + part_out.astype(jnp.float32)
        part_back = jnp.dot(d_gate[:, lower:upper], gate_w[lower:upper], preferred_element_type=jnp.float32)
        part_back = part_back + jnp.dot(d_up[:, lower:upper], up_w[lower:upper], preferred_element_type=jnp.float32)
        part_back = lax.optimization_barrier(part_back.astype(jnp.bfloat16))
        back_sum = back_sum + part_back.astype(jnp.float32)
    grad_down_e = jnp.dot(hidden.T, grad_slots, preferred_element_type=jnp.float32).astype(jnp.bfloat16)
    grad_gate_e = jnp.dot(d_gate.T, tok_slots, preferred_element_type=jnp.float32).astype(jnp.bfloat16)
    grad_up_e = jnp.dot(d_up.T, tok_slots, preferred_element_type=jnp.float32).astype(jnp.bfloat16)
    return out_sum.astype(jnp.bfloat16), back_sum.astype(jnp.bfloat16), grad_gate_e, grad_up_e, grad_down_e


def reference(tokens, expert_ids, router_probs, w_gate, w_up, w_down, out_grad):
    devices = N_DP * N_EXPERT
    per_device = TOK_DEV * TOPK
    id_table = expert_ids.reshape(devices, per_device).astype(jnp.int32)
    onehot = (id_table[:, :, None] == jnp.arange(EXPERTS, dtype=jnp.int32)[None, None, :]).astype(jnp.int32)
    rank_of = jnp.sum((jnp.cumsum(onehot, axis=1) - onehot) * onehot, axis=2).astype(jnp.int32)
    source = jnp.arange(devices, dtype=jnp.int32)[:, None]
    slot_index = ((id_table * devices + source) * MOST + rank_of).astype(jnp.int32)
    token_index = (source * TOK_DEV + jnp.arange(per_device, dtype=jnp.int32)[None, :] // TOPK).astype(jnp.int32)
    slot_total = EXPERTS * devices * MOST
    token_table = jnp.full((slot_total,), TOKENS, jnp.int32).at[slot_index.reshape(-1)].set(token_index.reshape(-1))
    weight_table = jnp.zeros((slot_total,), jnp.float32).at[slot_index.reshape(-1)].set(router_probs.reshape(-1).astype(jnp.float32))
    tok_pad = jnp.concatenate([tokens, jnp.zeros((1, D), jnp.bfloat16)], axis=0)
    grad_pad = jnp.concatenate([out_grad, jnp.zeros((1, D), jnp.bfloat16)], axis=0)

    def per_expert(inputs):
        table_e, prob_e, gate_w, up_w, down_w = inputs
        tok_slots = tok_pad[table_e]
        grad_slots = (prob_e[:, None] * grad_pad[table_e].astype(jnp.float32)).astype(jnp.bfloat16)
        return expert_pass(tok_slots, grad_slots, gate_w, up_w, down_w)

    outs_slots, back_slots, grad_gate, grad_up, grad_down = lax.map(
        per_expert,
        (token_table.reshape(EXPERTS, devices * MOST), weight_table.reshape(EXPERTS, devices * MOST), w_gate, w_up, w_down))
    out_flat = outs_slots.reshape(slot_total, D)
    back_flat = back_slots.reshape(slot_total, D)
    flat_slot = slot_index.reshape(TOKENS, TOPK)
    mixed = jnp.zeros((TOKENS, D), jnp.float32)
    input_grad = jnp.zeros((TOKENS, D), jnp.float32)
    grad_cols = []
    dy_float = out_grad.astype(jnp.float32)
    for k_index in range(TOPK):
        rows_k = out_flat[flat_slot[:, k_index]].astype(jnp.float32)
        mixed = mixed + router_probs[:, k_index:k_index + 1] * rows_k
        grad_cols.append(jnp.sum(dy_float * rows_k, axis=1))
        input_grad = input_grad + back_flat[flat_slot[:, k_index]].astype(jnp.float32)
    prob_grad = jnp.stack(grad_cols, axis=1)
    return (mixed.astype(jnp.bfloat16), input_grad.astype(jnp.bfloat16), prob_grad, grad_gate, grad_up, grad_down)
```

```python
import jax
import jax.numpy as jnp
from jax import lax
from jax.sharding import PartitionSpec as P


IN_CHUNKS = 2
OUT_CHUNKS = 2

BF = jnp.bfloat16
F32 = jnp.float32


def dot(a, b, dims):
    return lax.dot_general(a, b, ((dims[:1], dims[1:]), ((), ())), preferred_element_type=F32)


def exchange(blocks):
    n = len(blocks)
    return [blocks[0]] + [
        lax.ppermute(blocks[m], "expert", [(i, i ^ m) for i in range(n)]) for m in range(1, n)
    ]


def on_device(tokens, expert_ids, router_probs, w_gate, w_up, w_down, out_grad):
    tok_rows, width = tokens.shape
    top = expert_ids.shape[1]
    n_expert = lax.axis_size("expert")
    n_dp = lax.axis_size("dp")
    depth = max(2, tok_rows * top * 9 // (8 * n_expert))
    block = n_dp * depth
    total = n_expert * block
    me = lax.axis_index("expert").astype(jnp.int32)
    w_gate, w_up, w_down = w_gate[0], w_up[0], w_down[0]

    flat = expert_ids.reshape(-1)
    onehot = (flat[:, None] == jnp.arange(n_expert, dtype=jnp.int32)[None, :]).astype(jnp.int32)
    rank = jnp.sum((jnp.cumsum(onehot, axis=0) - onehot) * onehot, axis=1).reshape(tok_rows, top)
    dp_me = lax.axis_index("dp").astype(jnp.int32)
    row = (expert_ids ^ me) * block + dp_me * depth + rank
    meta = jnp.concatenate([row.astype(F32), router_probs], axis=1)
    meta = lax.all_gather(meta, "dp", axis=0, tiled=True)
    rows_t = meta[:, :top].astype(jnp.int32).T
    probs_t = meta[:, top:].astype(BF).T

    def selectors(m, weighted):
        r = lax.broadcasted_iota(jnp.int32, (block, 1), 0) + m * block
        out = jnp.zeros((block, rows_t.shape[1]), BF)
        for k in range(top):
            v = probs_t[k][None, :] if weighted else jnp.ones((), BF)
            out = out + jnp.where(rows_t[k][None, :] == r, v, jnp.zeros((), BF))
        return out

    sel = [selectors(m, False) for m in range(n_expert)]
    selp = [selectors(m, True) for m in range(n_expert)]

    def dispatch(x, s):
        parts = []
        step = width // IN_CHUNKS
        for c in range(IN_CHUNKS):
            whole = lax.all_gather(x[:, c * step : (c + 1) * step], "dp", axis=0, tiled=True)
            blocks = [dot(s[m], whole, (1, 0)).astype(BF) for m in range(n_expert)]
            parts.append(jnp.concatenate(exchange(blocks), axis=0))
        return parts

    def contract(parts, w):
        step = width // IN_CHUNKS
        out = dot(parts[0], w[:, :step], (1, 1))
        for c in range(1, IN_CHUNKS):
            out = out + dot(parts[c], w[:, c * step : (c + 1) * step], (1, 1))
        return out

    def weight_grad(left, parts):
        return jnp.concatenate([dot(left, p, (0, 0)).astype(BF) for p in parts], axis=1)[None]

    def send_back(rows_of, s):
        parts = []
        step = width // OUT_CHUNKS
        s_all = jnp.concatenate(s, axis=0)
        for c in range(OUT_CHUNKS):
            cols = slice(c * step, (c + 1) * step)
            blocks = [rows_of(slice(m * block, (m + 1) * block), cols) for m in range(n_expert)]
            back = jnp.concatenate(exchange(blocks), axis=0)
            mine = dot(s_all, back, (0, 0)).astype(BF)
            parts.append(lax.psum_scatter(mine, "dp", scatter_dimension=0, tiled=True))
        return jnp.concatenate(parts, axis=1)

    rows_in = dispatch(tokens, sel)
    grads_in = dispatch(out_grad, selp)

    gate = contract(rows_in, w_gate)
    up = contract(rows_in, w_up)
    sig = jax.nn.sigmoid(gate)
    act = gate * sig
    hidden_f = act * up
    hidden = hidden_f.astype(BF)
    mixed = send_back(lambda r, c: dot(hidden[r], w_down[:, c], (1, 0)).astype(BF), selp)

    d_hidden = contract(grads_in, w_down)
    d_gate = (d_hidden * up * sig * (1.0 + gate * (1.0 - sig))).astype(BF)
    d_up = (d_hidden * act).astype(BF)
    input_grad = send_back(
        lambda r, c: (
            dot(d_gate[r], w_gate[:, c], (1, 0)) + dot(d_up[r], w_up[:, c], (1, 0))
        ).astype(BF),
        sel,
    )

    scaled_pg = jnp.sum(hidden.astype(F32) * d_hidden, axis=1).reshape(n_expert, block)
    order = jnp.arange(n_expert, dtype=jnp.int32) ^ me
    pg = lax.all_to_all(scaled_pg[order], "expert", split_axis=0, concat_axis=0, tiled=True)
    pg = pg[order].reshape(-1)
    pg = jnp.stack(
        [
            jnp.sum(
                jnp.where(
                    rows_t[k][None, :] == lax.broadcasted_iota(jnp.int32, (total, 1), 0),
                    pg[:, None],
                    0.0,
                ),
                axis=0,
            )
            for k in range(top)
        ],
        axis=1,
    )
    pg = lax.psum_scatter(pg, "dp", scatter_dimension=0, tiled=True)
    prob_grad = pg / router_probs.astype(BF).astype(F32)

    grad_gate = weight_grad(d_gate, rows_in)
    grad_up = weight_grad(d_up, rows_in)
    grad_down = weight_grad(hidden, grads_in)
    return (mixed, input_grad, prob_grad, grad_gate, grad_up, grad_down)


def solution(mesh):
    tok = P(("dp", "expert"), None)
    wt = P("expert", "dp", None)
    return jax.shard_map(
        on_device,
        mesh=mesh,
        in_specs=(tok, tok, tok, wt, wt, wt, tok),
        out_specs=(tok, tok, tok, wt, wt, wt),
        check_vma=False,
    )
```

```python
import jax
import jax.numpy as jnp
from jax import lax
from jax.sharding import PartitionSpec as P


IN_PARTS = (8, 8)
MIX_PARTS = (8, 8)
DX_PARTS = (8, 4, 4)

EARLY = True

BF = jnp.bfloat16
F32 = jnp.float32


def dot(a, b, dims):
    return lax.dot_general(a, b, ((dims[:1], dims[1:]), ((), ())), preferred_element_type=F32)


def exchange(blocks):
    n = len(blocks)
    return [blocks[0]] + [
        lax.ppermute(blocks[m], "expert", [(i, i ^ m) for i in range(n)]) for m in range(1, n)
    ]


def on_device(tokens, expert_ids, router_probs, w_gate, w_up, w_down, out_grad):
    tok_rows, width = tokens.shape
    top = expert_ids.shape[1]
    n_expert = lax.axis_size("expert")
    n_dp = lax.axis_size("dp")
    depth = max(2, tok_rows * top * 9 // (8 * n_expert))
    block = n_dp * depth
    total = n_expert * block
    me = lax.axis_index("expert").astype(jnp.int32)
    w_gate, w_up, w_down = w_gate[0], w_up[0], w_down[0]

    flat = expert_ids.reshape(-1)
    onehot = (flat[:, None] == jnp.arange(n_expert, dtype=jnp.int32)[None, :]).astype(jnp.int32)
    rank = jnp.sum((jnp.cumsum(onehot, axis=0) - onehot) * onehot, axis=1).reshape(tok_rows, top)
    dp_me = lax.axis_index("dp").astype(jnp.int32)
    row = (expert_ids ^ me) * block + dp_me * depth + rank
    meta = jnp.concatenate([row.astype(F32), router_probs], axis=1)
    meta = lax.all_gather(meta, "dp", axis=0, tiled=True)
    rows_t = meta[:, :top].astype(jnp.int32).T
    probs_t = meta[:, top:].astype(BF).T

    def selector(values):
        r = lax.broadcasted_iota(jnp.int32, (total, 1), 0)
        out = jnp.zeros((total, rows_t.shape[1]), BF)
        for k in range(top):
            out = out + jnp.where(rows_t[k][None, :] == r, values[k], jnp.zeros((), BF))
        return out

    sel = selector([jnp.ones((), BF)] * top)
    selp = selector([probs_t[k][None, :] for k in range(top)])

    def columns(parts):
        edges = [0]
        for p in parts:
            edges.append(edges[-1] + p * width // 16)
        return [slice(lo, hi) for lo, hi in zip(edges[:-1], edges[1:])]

    def split(rows):
        return [rows[m * block : (m + 1) * block] for m in range(n_expert)]

    def gather(x):
        return [lax.all_gather(x[:, c], "dp", axis=0, tiled=True) for c in columns(IN_PARTS)]

    def dispatch(whole, s):
        return jnp.concatenate(exchange(split(dot(s, whole, (1, 0)).astype(BF))), axis=0)

    def contract(parts, w):
        out = None
        for part, c in zip(parts, columns(IN_PARTS)):
            term = dot(part, w[:, c], (1, 1))
            out = term if out is None else out + term
        return out

    def weight_grad(left, parts):
        return jnp.concatenate([dot(left, p, (0, 0)).astype(BF) for p in parts], axis=1)[None]

    def send_back(rows, s):
        back = jnp.concatenate(exchange(split(rows)), axis=0)
        mine = dot(s, back, (0, 0)).astype(BF)
        return lax.psum_scatter(mine, "dp", scatter_dimension=0, tiled=True)

    tok_parts = gather(tokens)
    og_parts = gather(out_grad)
    rows_in = [dispatch(x, sel) for x in tok_parts]
    grads_in = [dispatch(x, selp) for x in og_parts[:-1]]

    gate = contract(rows_in, w_gate)
    up = contract(rows_in, w_up)
    sig = jax.nn.sigmoid(gate)
    act = gate * sig
    hidden = (act * up).astype(BF)
    mixed_rows = [dot(hidden, w_down[:, c], (1, 0)).astype(BF) for c in columns(MIX_PARTS)]
    if EARLY:
        last, _ = lax.optimization_barrier((og_parts[-1], mixed_rows[0]))
    else:
        last = og_parts[-1]
    grads_in.append(dispatch(last, selp))
    mixed = jnp.concatenate([send_back(r, selp) for r in mixed_rows], axis=1)

    d_hidden = contract(grads_in, w_down)
    d_gate = (d_hidden * up * sig * (1.0 + gate * (1.0 - sig))).astype(BF)
    d_up = (d_hidden * act).astype(BF)
    d_both = jnp.concatenate([d_gate, d_up], axis=1)
    w_both = jnp.concatenate([w_gate, w_up], axis=0)
    input_grad = jnp.concatenate(
        [
            send_back(dot(d_both, w_both[:, c], (1, 0)).astype(BF), sel)
            for c in columns(DX_PARTS)
        ],
        axis=1,
    )

    scaled_pg = jnp.sum(hidden.astype(F32) * d_hidden, axis=1).reshape(n_expert, block)
    order = jnp.arange(n_expert, dtype=jnp.int32) ^ me
    pg = lax.all_to_all(scaled_pg[order], "expert", split_axis=0, concat_axis=0, tiled=True)
    pg = pg[order].reshape(-1)
    slots = lax.broadcasted_iota(jnp.int32, (total, 1), 0)
    pg = jnp.stack(
        [
            jnp.sum(jnp.where(rows_t[k][None, :] == slots, pg[:, None], 0.0), axis=0)
            for k in range(top)
        ],
        axis=1,
    ).reshape(n_dp, tok_rows, top)
    own = lax.dynamic_index_in_dim(pg, dp_me, 0, keepdims=False)
    for turn in range(1, n_dp):
        theirs = lax.dynamic_index_in_dim(pg, (dp_me + turn) % n_dp, 0, keepdims=False)
        own = own + lax.ppermute(theirs, "dp", [(i, (i + turn) % n_dp) for i in range(n_dp)])
    prob_grad = own / router_probs.astype(BF).astype(F32)

    grad_gate = weight_grad(d_gate, rows_in)
    grad_up = weight_grad(d_up, rows_in)
    grad_down = weight_grad(hidden, grads_in)
    return (mixed, input_grad, prob_grad, grad_gate, grad_up, grad_down)


def solution(mesh):
    tok = P(("dp", "expert"), None)
    wt = P("expert", "dp", None)
    return jax.shard_map(
        on_device,
        mesh=mesh,
        in_specs=(tok, tok, tok, wt, wt, wt, tok),
        out_specs=(tok, tok, tok, wt, wt, wt),
        check_vma=False,
    )
```
